128 devices in a mesh: row: 8 (over z, core), col: 16 (over x, y).
Axes of the slice: x: 4, y: 4, z: 4, core: 2. Of those that a mesh axis runs over, the one named last changes fastest.
Arguments:
- velocity: float32 [2, 512, 128, 384], P(None, 'col', 'row'), may hold values from -6 to 6
- synthesis: float32 [384, 384], replicated
- analysis: float32 [384, 384], replicated
- radial_eigen: float32 [384], replicated, may hold values from 0.05 to 4
- pair_list: int32 [256, 2], replicated, may hold values from 0 to 511, as said below
- owner_slot: int32 [256], replicated, may hold values from 0 to 255, each once
- freq_list: int32 [4], replicated, may hold values from 0 to 255
- snap_index: int32 [1], replicated, may hold values from 0 to 254
- block_dft: float32 [256, 4, 2, 384], P(('row', 'col')), may hold values from -6 to 6
- spectra: float32 [256, 4, 2, 384, 384], P(('row', 'col')), may hold values from -6 to 6
Outputs:
- velocity_next: float32 [2, 512, 128, 384], P(None, 'col', 'row')
- block_sums: float32 [256, 4, 2, 384], P(('row', 'col'))
- spectra_next: float32 [256, 4, 2, 384, 384], P(('row', 'col'))
The draws below stay inside these ranges and needn't reach their ends.
Inputs may be any that keep to these rules, and one draw needn't show every extreme that they name: `pair_list`: the pairs are distinct; the axial index is below 128 and the wavenumber below 512. Of the devices of the solver layout (row index times the size of col plus col index, holding axial indices row * 16 onward and wavenumbers col * 512 / size of col onward), each holds at most 8 selected pairs and some hold exactly 8. `owner_slot`: each slot once.
All inputs are finite; a program needn't handle non-finite values.
Results may differ from the reference program's by a relative error of at most 0.0001.
Values sent between devices are 32-bit elements; how exact they have to be, the bound alone decides.
No kernel may reach another device: no remote copies, remote signals or barrier semaphores. Data moves between devices by JAX's collectives and lax.ppermute only.
A program may use at most 128 MiB of HBM per device.

```python
import math
import jax
import jax.numpy as jnp
from jax import lax

KX_DEV = 16
MTH = 512
NR = 384
SLOTS = 2
NFREQ = 4
NBLK = 256
NTH = 1536
NKX = 128
NSEL = 256
HOLD = 8
DEVICES = 128


def near_identity(key):
    spread = jax.random.normal(key, (NR, NR), jnp.float32) * (0.3 / NR ** 0.5)
    return jnp.eye(NR, dtype=jnp.float32) + spread


def draw_synthesis(key, part):
    return near_identity(jax.random.fold_in(key, 21))


def draw_analysis(key, part):
    return near_identity(jax.random.fold_in(key, 22))


def draw_pair_list(key, part):
    base = jax.random.fold_in(key, 31)
    order_key, cell_key, shuffle_key = jax.random.split(base, 3)
    col_count = DEVICES // (NKX // KX_DEV)
    modes_dev = MTH // col_count
    cells_each = KX_DEV * modes_dev
    device_order = jax.random.permutation(order_key, DEVICES)
    busy_count = DEVICES // 8
    first_block = busy_count * HOLD
    listing = jnp.arange(NSEL, dtype=jnp.int32)
    later = jnp.maximum(listing - first_block, 0)
    rank_of = jnp.where(listing < first_block, listing // HOLD, busy_count + later // (2 * SLOTS))
    within = jnp.where(listing < first_block, listing % HOLD, later % (2 * SLOTS))
    holder = device_order[rank_of]

    def first_cells(cell_one):
        return jax.random.permutation(cell_one, cells_each)[:HOLD]
    chosen = jax.vmap(first_cells)(jax.random.split(cell_key, DEVICES))
    cell = chosen[holder, within]
    axial = holder // col_count * KX_DEV + cell // modes_dev
    mode = holder % col_count * modes_dev + cell % modes_dev
    pairs = jnp.stack([axial, mode], axis=1).astype(jnp.int32)
    return pairs[jax.random.permutation(shuffle_key, NSEL)]


def touch_ends(array, stream_key, least, high):
    longest = array.shape.index(max(array.shape))
    spots = []
    for shift in (0, 1):
        where = [jax.random.randint(jax.random.fold_in(stream_key, axis), (), 0, length) for axis, length in enumerate(array.shape)]
        where[longest] = (where[longest] + shift) % array.shape[longest]
        spots.append(tuple(where))
    return array.at[spots[0]].set(least).at[spots[1]].set(high)


def level_of(key, dims, cuts, low, largest):
    def one(axis_at, parts):
        steps = jax.random.uniform(jax.random.fold_in(jax.random.fold_in(key, 6), axis_at), (parts,), jnp.float32, low / len(cuts), largest / len(cuts))
        return jnp.repeat(jnp.exp(steps), dims[axis_at] // parts).reshape((-1,) + (1,) * (len(dims) - axis_at - 1))

    factor_of = one(*cuts[0])
    for cut in cuts[1:]:
        factor_of = factor_of * one(*cut)
    return factor_of


def bell_draw(own_key, dims, width, reach, pieces=(), kind=jnp.bfloat16):
    entries = width * jax.random.normal(own_key, dims, jnp.float32)
    if pieces:
        entries = entries * level_of(own_key, dims, pieces, -0.22, 0.18)
    return jnp.clip(entries, -reach, reach).astype(kind)


def setup_inputs(seed: int = 0) -> dict:
    streams_of = jax.random.split(jax.random.key(seed), 11)
    velocity = bell_draw(streams_of[0], (2, MTH, NKX, NR), 1.0, 6.0, ((1, 16), (2, 8)), jnp.float32)
    synthesis = draw_synthesis(jax.random.fold_in(streams_of[10], 71), 0)
    analysis = draw_analysis(jax.random.fold_in(streams_of[10], 71), 0)
    radial_eigen = jnp.clip(jnp.exp(jax.random.uniform(streams_of[3], (NR,), jnp.float32, math.log(0.05), math.log(4.0))), 0.05, 4.0)
    pair_list = draw_pair_list(jax.random.fold_in(streams_of[10], 71), 0)
    owner_slot = jax.random.permutation(streams_of[5], NSEL).astype(jnp.int32)
    freq_list = touch_ends(jax.random.randint(streams_of[6], (NFREQ,), 0, NBLK), jax.random.fold_in(streams_of[6], 1), 0, NBLK - 1).astype(jnp.int32)
    snap_index = jax.random.randint(streams_of[7], (1,), 0, NBLK - 1).astype(jnp.int32)
    block_dft = bell_draw(streams_of[8], (NSEL, NFREQ, 2, NR), 1.0, 6.0, ((0, 128),), jnp.float32)
    spectra = bell_draw(streams_of[9], (NSEL, NFREQ, 2, NR, NR), 1.0, 6.0, ((0, 128),), jnp.float32)
    return dict(velocity=velocity, synthesis=synthesis, analysis=analysis, radial_eigen=radial_eigen, pair_list=pair_list, owner_slot=owner_slot, freq_list=freq_list, snap_index=snap_index, block_dft=block_dft, spectra=spectra)


viscosity = 4e-06
axial_scale = 2.0
nonlinear_gain = 0.1
highest = lax.Precision.HIGHEST

def circle_forcing(current):
    spectrum = current[0] + 1j * current[1]
    physical = jnp.fft.irfft(spectrum, n=NTH, axis=0) * (NTH / math.sqrt(MTH))
    squared = physical * physical
    folded = jnp.fft.rfft(squared, axis=0)[:MTH] * (math.sqrt(MTH) / NTH)
    keep_mask = (jnp.arange(MTH) > 0)[:, None, None]
    real_part = jnp.where(keep_mask, folded.real, 0.0)
    imag_part = jnp.where(keep_mask, folded.imag, 0.0)
    return jnp.stack([real_part, imag_part]).astype(jnp.float32)

def radial_solve(rhs, analysis, synthesis, damping):
    coeffs = jnp.einsum('cmkr,rq->cmkq', rhs, analysis, precision=highest) * damping[None]
    return jnp.einsum('cmkq,qs->cmks', coeffs, synthesis, precision=highest)

def window_terms(freq_list, snap_now):
    position = snap_now.astype(jnp.float32)
    window = 0.54 - 0.46 * jnp.cos(2.0 * math.pi * position / NBLK)
    phase = (freq_list * snap_now % NBLK).astype(jnp.float32) * (2.0 * math.pi / NBLK)
    return (window * jnp.cos(phase), -window * jnp.sin(phase))

def add_snapshot(block, snapshot, real_w, imag_w):
    real_new = block[:, :, 0] + real_w[None, :, None] * snapshot[0][:, None, :] - imag_w[None, :, None] * snapshot[1][:, None, :]
    imag_new = block[:, :, 1] + real_w[None, :, None] * snapshot[1][:, None, :] + imag_w[None, :, None] * snapshot[0][:, None, :]
    return jnp.stack([real_new, imag_new], axis=2)

def spectral_update(spectrum_one, old_block, new_block):
    old_real, old_imag = (old_block[:, 0], old_block[:, 1])
    new_real, new_imag = (new_block[:, 0], new_block[:, 1])
    left_real = jnp.stack([new_real, new_imag, old_real, old_imag], axis=1)
    left_imag = jnp.stack([new_imag, -new_real, old_imag, -old_real], axis=1)
    left = jnp.stack([left_real, left_imag], axis=1)
    right = jnp.stack([new_real, new_imag, -old_real, -old_imag], axis=1)
    return spectrum_one + jnp.einsum('fckr,fkq->fcrq', left, right, precision=highest)

def slot_update(items):
    return spectral_update(items[0], items[1], items[2])

def reference(velocity, synthesis, analysis, radial_eigen, pair_list, owner_slot, freq_list, snap_index, block_dft, spectra):
    axial_ids = jnp.arange(NKX).astype(jnp.float32) * axial_scale
    mode_ids = jnp.arange(MTH).astype(jnp.float32)
    damping = 1.0 / (1.0 + viscosity * (axial_ids[None, :, None] ** 2 + mode_ids[:, None, None] ** 2) + radial_eigen[None, None, :])
    current = velocity
    snapshots = []
    for section_index in range(2):
        rhs = current - nonlinear_gain * circle_forcing(current)
        current = radial_solve(rhs, analysis, synthesis, damping)
        snapshots.append(current)
    slot_ids = jnp.arange(NSEL, dtype=jnp.int32)
    pair_of_slot = jnp.zeros((NSEL,), jnp.int32).at[owner_slot].set(slot_ids)
    axial_sel = pair_list[pair_of_slot, 0].astype(jnp.int32)
    mode_sel = pair_list[pair_of_slot, 1].astype(jnp.int32)
    block = block_dft
    for section_index in range(2):
        picked = snapshots[section_index][:, mode_sel, axial_sel, :]
        real_w, imag_w = window_terms(freq_list, snap_index[0] + section_index)
        block = add_snapshot(block, picked, real_w, imag_w)
    spectra_next = lax.map(slot_update, (spectra, block_dft, block))
    return (current, block, spectra_next)
```

```python
import math

import jax
import jax.numpy as jnp
from jax import lax
from jax.experimental import pallas as pl
from jax.experimental.pallas import tpu as pltpu
from jax.sharding import PartitionSpec as P


NBLK = 256
MTH = 512
NTH = 1536
NR = 384
HALF = MTH // 2
QUARTER = NTH // 4

viscosity = 4e-06
axial_scale = 2.0
nonlinear_gain = 0.1

f32 = jnp.float32
bf16 = jnp.bfloat16


SYNTH_WEIGHT = 2.0 / math.sqrt(MTH)
KEEP = math.sqrt(MTH) / NTH
VMEM = pl.BlockSpec(memory_space=pltpu.VMEM)
SMEM = pl.BlockSpec(memory_space=pltpu.SMEM)
HBM = pl.BlockSpec(memory_space=pltpu.HBM)
ANY = pl.BlockSpec(memory_space=pl.ANY)


def in_hbm(array):
    return pltpu.with_memory_space_constraint(array, pltpu.HBM)


def params(mib):
    return pltpu.CompilerParams(vmem_limit_bytes=mib << 20)


def trig_tables(transposed):
    dims = (4, HALF, QUARTER) if transposed else (4, QUARTER, HALF)
    mode_dim, point_dim = (1, 2) if transposed else (2, 1)
    kind = lax.broadcasted_iota(jnp.int32, dims, 0)
    mode = (2 * lax.broadcasted_iota(jnp.int32, dims, mode_dim) + (kind & 1)).astype(f32)
    point = (2 * lax.broadcasted_iota(jnp.int32, dims, point_dim) + 1).astype(f32)
    product = mode * point - jnp.where(kind >= 2, NTH / 2.0, 0.0)
    turn = product - jnp.round(product * (0.5 / NTH)) * (2.0 * NTH)
    quarter = (NTH / 2.0 - jnp.abs(turn)) * (math.pi / NTH)
    square = quarter * quarter
    series = 1.0 / math.factorial(13)
    for power in (11, 9, 7, 5, 3, 1):
        series = (1.0 if power % 4 == 1 else -1.0) / math.factorial(power) + square * series
    table = quarter * series
    high = lax.reduce_precision(table, 8, 7)
    low = table - high
    high, low = high.astype(bf16), low.astype(bf16)
    return high, low


def gather_kernel(src_ref, out_ref):
    for parity in range(2):
        block = jnp.stack([src_ref[0, 2 * i + parity] for i in range(8)])
        out_ref[:, parity * 8 : parity * 8 + 8, :] = pltpu.einshape("mar->amr", block)


def to_axial_major(velocity):
    return pl.pallas_call(
        gather_kernel,
        out_shape=jax.ShapeDtypeStruct((16, 64, NR), f32),
        grid=(2, 2),
        in_specs=[pl.BlockSpec((1, 16, 16, NR), lambda c, i: (c, i, 0, 0))],
        out_specs=pl.BlockSpec((16, 16, NR), lambda c, i: (0, 2 * c + i, 0)),
        compiler_params=params(8),
        cost_estimate=pl.CostEstimate(flops=0, bytes_accessed=2 * 1024 * NR * 4, transcendentals=0),
        name="axial_major",
    )(in_hbm(velocity))


def scatter_kernel(src_ref, out_ref):
    for parity in range(2):
        block = src_ref[:, parity * 8 : parity * 8 + 8, :]
        moved = pltpu.einshape("amr->mar", block)
        for i in range(8):
            out_ref[0, 2 * i + parity] = moved[i]


def from_axial_major(moved):
    return pl.pallas_call(
        scatter_kernel,
        out_shape=jax.ShapeDtypeStruct((2, 32, 16, NR), f32),
        grid=(2, 2),
        in_specs=[pl.BlockSpec((16, 16, NR), lambda c, i: (0, 2 * c + i, 0))],
        out_specs=pl.BlockSpec((1, 16, 16, NR), lambda c, i: (c, i, 0, 0)),
        compiler_params=params(8),
        cost_estimate=pl.CostEstimate(flops=0, bytes_accessed=2 * 1024 * NR * 4, transcendentals=0),
        name="mode_major",
    )(moved)


def list_kernel(pair_ref, owner_ref, place_ref, count_ref, spot_ref, mode_ref):
    mine, core, z, x, y = (place_ref[i] for i in range(5))

    def eight(b, n):
        for u in range(8):
            mode_ref[n] = b * 8 + u
            n = n + jnp.where(pair_ref[0, b * 8 + u] == mine, 1, 0)
        return n

    def place_one(k, carry):
        i = mode_ref[k]
        slot = owner_ref[i]
        row, col = slot // 32, (slot // 2) & 15
        spot_ref[k] = (
            ((row & 1) ^ core) * 128
            + (((row >> 1) - z) & 3) * 32
            + (((col >> 2) - x) & 3) * 8
            + (((col & 3) - y) & 3) * 2
            + (slot & 1)
        )
        mode_ref[k] = pair_ref[1, i]
        return carry

    count = lax.fori_loop(0, 32, eight, 0)
    count_ref[0] = count
    lax.fori_loop(0, count, place_one, 0)


def pair_lists(pair_list, owner_slot, place):
    return pl.pallas_call(
        list_kernel,
        out_shape=(
            jax.ShapeDtypeStruct((1,), jnp.int32),
            jax.ShapeDtypeStruct((257,), jnp.int32),
            jax.ShapeDtypeStruct((257,), jnp.int32),
        ),
        in_specs=[SMEM] * 3,
        out_specs=[SMEM] * 3,
        compiler_params=params(1),
        cost_estimate=pl.CostEstimate(flops=0, bytes_accessed=8000000, transcendentals=0),
        name="pair_lists",
    )(pair_list.T, owner_slot, place)


def split(value):
    high = value.astype(bf16)
    return high, (value - high.astype(f32)).astype(bf16)


BANDS = ((0, 256), (256, 128))


def steps_kernel(
    count_ref,
    spot_ref,
    mode_ref,
    moved_any,
    synth_any,
    anal_any,
    analysis_any,
    synthesis_any,
    damp_any,
    out_any,
    keep_any,
    send_any,
    state,
    synth_ref,
    anal_ref,
    analysis_ref,
    synthesis_ref,
    damp_ref,
    cols,
    phys,
    squares,
    rows,
    parcel,
    sems,
):
    def strip(array, part, half):
        return array.at[:, pl.ds((part // 2) * 32 + half * 16 + (part % 2) * 8, 8), :]

    def held(part, half):
        return state.at[part, :, pl.ds(half * 8, 8), :]

    moved_in = [
        [
            pltpu.make_async_copy(strip(moved_any, part, half), held(part, half), sems.at[2 * part + half])
            for half in range(2)
        ]
        for part in range(4)
    ]
    synth_in = [
        pltpu.make_async_copy(synth_any.at[part], synth_ref.at[part], sems.at[8 + part]) for part in range(4)
    ]
    anal_in = [pltpu.make_async_copy(anal_any.at[part], anal_ref.at[part], sems.at[12 + part]) for part in range(4)]
    rest_in = [
        pltpu.make_async_copy(analysis_any, analysis_ref, sems.at[16]),
        pltpu.make_async_copy(damp_any, damp_ref, sems.at[17]),
        pltpu.make_async_copy(synthesis_any, synthesis_ref, sems.at[18]),
    ]
    for part in range(4):
        for copy in moved_in[part]:
            copy.start()
        synth_in[part].start()
    for copy in anal_in + rest_in:
        copy.start()
    parcel[...] = jnp.zeros_like(parcel)

    def store_rows(at, lanes, value):
        high, low = split(value)
        start, width = lanes
        rows[at, start : start + width] = high
        rows[at, NR + start : NR + start + width] = low
        rows[at, 2 * NR + start : 2 * NR + start + width] = high

    def step(t, carry):
        for start, width in BANDS:
            lanes = pl.ds(start, width)
            for part in range(4):
                if start == 0:

                    @pl.when(t == 0)
                    def _():
                        for copy in moved_in[part]:
                            copy.wait()
                        synth_in[part].wait()

                for b in range(0, HALF, 64):
                    scaled = state[part, pl.ds(b // 16, 4), :, lanes].reshape(64, width) * SYNTH_WEIGHT
                    if part == 0 and b == 0:
                        first_row = lax.broadcasted_iota(jnp.int32, scaled.shape, 0) == 0
                        scaled = jnp.where(first_row, 0.5 * scaled, scaled)
                    high, low = split(scaled)
                    cols[part, pl.ds(b, 64), lanes] = high
                    cols[part, pl.ds(HALF + b, 64), lanes] = low
                    cols[part, pl.ds(2 * HALF + b, 64), lanes] = high
                phys[part, :, lanes] = jnp.dot(synth_ref[part], cols[part, :, lanes], preferred_element_type=f32)

        @pl.when(t == 0)
        def _():
            for copy in anal_in + rest_in:
                copy.wait()

        for start, width in BANDS:
            lanes = pl.ds(start, width)
            for b in range(0, QUARTER, 32):
                ce, co, se, so = (phys[part, pl.ds(b, 32), lanes] for part in range(4))
                a, b_, s, d = ce + co, ce - co, se + so, se - so
                near, far = a * a + s * s, b_ * b_ + d * d
                near_x, far_x = a * s, b_ * d
                for part, value in enumerate((near + far, near - far, near_x + far_x, near_x - far_x)):
                    high, low = split(value)
                    squares[part, pl.ds(b, 32), lanes] = high
                    squares[part, pl.ds(QUARTER + b, 32), lanes] = low
                    squares[part, pl.ds(2 * QUARTER + b, 32), lanes] = high
            for part in range(4):
                folded = jnp.dot(anal_ref[part], squares[part, :, lanes], preferred_element_type=f32)
                gain = -nonlinear_gain * KEEP * (2.0 if part < 2 else 4.0)
                if part == 0:
                    first_row = lax.broadcasted_iota(jnp.int32, folded.shape, 0) == 0
                    folded = jnp.where(first_row, 0.0, folded)
                old = state[part, :, :, lanes].reshape(HALF, width)
                store_rows(pl.ds(part * HALF, HALF), (start, width), old + gain * folded)
        for half in range(2):
            at = pl.ds(half * MTH, MTH)
            coeffs = jnp.dot(rows[at, :], analysis_ref[...], preferred_element_type=f32)
            store_rows(at, (0, NR), coeffs * damp_ref[...])
        for half in range(2):
            at = pl.ds(half * MTH, MTH)
            value = jnp.dot(rows[at, :], synthesis_ref[...], preferred_element_type=f32)
            state[pl.ds(2 * half, 2)] = value.reshape(2, 16, 16, NR)
        return carry

    def pick(t):
        def one(i, carry):
            mode = mode_ref[i]
            part, group, row = mode & 1, (mode >> 1) >> 4, (mode >> 1) & 15
            dst = spot_ref[i] * 4 + 2 * t
            parcel[pl.ds(dst, 1), :] = state[part, group, pl.ds(row, 1), :]
            parcel[pl.ds(dst + 1, 1), :] = state[part + 2, group, pl.ds(row, 1), :]
            return carry

        lax.fori_loop(0, count_ref[0], one, 0)

    def step_and_pick(t, carry):
        step(t, 0)
        pick(t)
        return carry

    lax.fori_loop(0, 2, step_and_pick, 0)
    copies = [
        pltpu.make_async_copy(held(part, half), strip(out_any, part, half), sems.at[2 * part + half])
        for part in range(4)
        for half in range(2)
    ]
    copies.append(pltpu.make_async_copy(parcel.at[pl.ds(512, 512)], send_any, sems.at[8]))
    copies.append(pltpu.make_async_copy(parcel.at[pl.ds(0, 512)], keep_any, sems.at[9]))
    for copy in copies:
        copy.start()
    for copy in copies:
        copy.wait()


def two_steps(lists, moved, synth, anal, analysis, synthesis, damping):
    return pl.pallas_call(
        steps_kernel,
        out_shape=(
            pltpu.HBM((16, 64, NR), f32),
            pltpu.HBM((512, NR), f32),
            pltpu.HBM((512, NR), f32),
        ),
        in_specs=[SMEM] * 3 + [ANY] + [HBM] * 5,
        out_specs=[HBM, HBM, HBM],
        scratch_shapes=[
            pltpu.VMEM((4, 16, 16, NR), f32),
            pltpu.VMEM((4, QUARTER, 3 * HALF), bf16),
            pltpu.VMEM((4, HALF, 3 * QUARTER), bf16),
            pltpu.VMEM((3 * NR, NR), bf16),
            pltpu.VMEM((3 * NR, NR), bf16),
            pltpu.VMEM((MTH, NR), f32),
            pltpu.VMEM((4, 3 * HALF, NR), bf16),
            pltpu.VMEM((4, QUARTER, NR), f32),
            pltpu.VMEM((4, 3 * QUARTER, NR), bf16),
            pltpu.VMEM((1024, 3 * NR), bf16),
            pltpu.VMEM((1024, NR), f32),
            pltpu.SemaphoreType.DMA((19,)),
        ],
        compiler_params=params(40),
        cost_estimate=pl.CostEstimate(flops=8_000_000_000, bytes_accessed=10_000_000, transcendentals=0),
        name="two_steps",
    )(*lists, moved, *map(in_hbm, (synth, anal, analysis, synthesis, damping)))


def products(lefts, rights, left, right):
    def three(value):
        high = value.astype(bf16).astype(f32)
        middle = (value - high).astype(bf16).astype(f32)
        return high, middle, (value - high - middle).astype(bf16).astype(f32)

    pairs = ((0, 0), (0, 1), (1, 0), (1, 1), (0, 2), (2, 0))
    left[...] = jnp.zeros_like(left)
    right[...] = jnp.zeros_like(right)
    count = len(rights)
    for k in range(count):
        for part in range(2):
            pieces = three(lefts[k][part])
            for p, (i, _) in enumerate(pairs):
                left[p * count + k : p * count + k + 1, part * NR : (part + 1) * NR] = pieces[i]
        pieces = three(rights[k])
        for p, (_, i) in enumerate(pairs):
            right[p * count + k : p * count + k + 1, :] = pieces[i]
    r = right[...].astype(bf16)
    for part in range(2):
        l = left[:, part * NR : (part + 1) * NR].T.astype(bf16)
        yield part, jnp.dot(l, r, preferred_element_type=f32)


def retire_kernel(block_ref, spectra_ref, out_ref, left, right):
    step = pl.program_id(0)
    real, imag = block_ref[0, 0:1, :], block_ref[0, 1:2, :]
    for part, value in products(((real, imag), (imag, -real)), (real, imag), left, right):
        out_ref[step, part] = spectra_ref[0, part] - value


def retire_old(block_dft, spectra):
    return pl.pallas_call(
        retire_kernel,
        out_shape=jax.ShapeDtypeStruct((8, 2, NR, NR), f32),
        grid=(8,),
        in_specs=[
            pl.BlockSpec((1, 2, NR), lambda i: (i, 0, 0)),
            pl.BlockSpec((1, 2, NR, NR), lambda i: (i, 0, 0, 0)),
        ],
        out_specs=VMEM,
        scratch_shapes=[pltpu.VMEM((16, 2 * NR), f32), pltpu.VMEM((16, NR), f32)],
        compiler_params=params(16),
        cost_estimate=pl.CostEstimate(flops=300_000_000, bytes_accessed=19_000_000, transcendentals=0),
        name="retire_old",
    )(block_dft.reshape(8, 2, NR), in_hbm(spectra.reshape(8, 2, NR, NR)))


def admit_kernel(weight_ref, snap_ref, block_ref, retired_ref, sums_ref, out_any, spread, sems):
    real, imag = block_ref[:, 0, :], block_ref[:, 1, :]
    for t in range(2):
        real_w, imag_w = weight_ref[:, 2 * t : 2 * t + 1], weight_ref[:, 2 * t + 1 : 2 * t + 2]
        snap_real, snap_imag = (
            jnp.concatenate(
                [
                    jnp.broadcast_to(snap_ref[slot * 4 + 2 * t + c : slot * 4 + 2 * t + c + 1, :], (4, NR))
                    for slot in range(2)
                ],
                axis=0,
            )
            for c in range(2)
        )
        real, imag = (
            real + real_w * snap_real - imag_w * snap_imag,
            imag + real_w * snap_imag + imag_w * snap_real,
        )
    sums_ref[:, 0, :] = real
    sums_ref[:, 1, :] = imag
    real_cols, imag_cols = real.T, imag.T
    copies = []
    rows = NR // 2
    for i in range(8):
        for half in range(2):
            n = 2 * i + half
            held = n % 8
            if n >= 8:
                copies[n - 8].wait()
            for b in range(0, rows, 32):
                at, here = pl.ds(half * rows + b, 32), pl.ds(b, 32)
                cr = real_cols[half * rows + b : half * rows + b + 32, i : i + 1]
                ci = imag_cols[half * rows + b : half * rows + b + 32, i : i + 1]
                rr, ri = real[i : i + 1, :], imag[i : i + 1, :]
                spread[held, 0, here, :] = retired_ref[i, 0, at, :] + (cr * rr + ci * ri)
                spread[held, 1, here, :] = retired_ref[i, 1, at, :] + (ci * rr - cr * ri)
            copies.append(
                pltpu.make_async_copy(
                    spread.at[held], out_any.at[i, :, pl.ds(half * rows, rows), :], sems.at[n]
                )
            )
            copies[n].start()
    for n in range(8, 16):
        copies[n].wait()


def admit_new(weights, snaps, block_dft, retired):
    sums, out = pl.pallas_call(
        admit_kernel,
        out_shape=(
            jax.ShapeDtypeStruct((8, 2, NR), f32),
            jax.ShapeDtypeStruct((8, 2, NR, NR), f32),
        ),
        in_specs=[VMEM] * 4,
        out_specs=[VMEM, ANY],
        scratch_shapes=[pltpu.VMEM((8, 2, NR // 2, NR), f32), pltpu.SemaphoreType.DMA((16,))],
        compiler_params=params(8),
        cost_estimate=pl.CostEstimate(flops=300_000_000, bytes_accessed=10_000_000, transcendentals=0),
        name="admit_new",
    )(weights, snaps, block_dft.reshape(8, 2, NR), retired)
    return sums.reshape(2, 4, 2, NR), out.reshape(2, 4, 2, NR, NR)


def window_terms(freq_list, snap_now):
    position = snap_now.astype(f32)
    window = 0.54 - 0.46 * jnp.cos(2.0 * math.pi * position / NBLK)
    phase = (freq_list * snap_now % NBLK).astype(f32) * (2.0 * math.pi / NBLK)
    return (window * jnp.cos(phase), -window * jnp.sin(phase))


def route(keep, send):
    rows = [[z * 2 + c for c in range(2)] for z in range(4)]
    got = lax.ppermute(send, "row", [(i, i ^ 1) for i in range(8)])
    z_size = 128
    blocks = [keep[k * z_size : (k + 1) * z_size] + got[k * z_size : (k + 1) * z_size] for k in range(4)]

    def turn(blocks, axis, pairs_of):
        total = blocks[0]
        for k in range(1, 4):
            moved = lax.ppermute(blocks[k], axis, pairs_of(k))
            total = total + moved
        return total

    total = turn(blocks, "row", lambda k: [(rows[z][c], rows[(z + k) % 4][c]) for z in range(4) for c in range(2)])
    blocks = [total[k * 32 : (k + 1) * 32] for k in range(4)]
    total = turn(blocks, "col", lambda k: [(x * 4 + y, (x + k) % 4 * 4 + y) for x in range(4) for y in range(4)])
    blocks = [total[k * 8 : (k + 1) * 8] for k in range(4)]
    snaps = turn(blocks, "col", lambda k: [(x * 4 + y, x * 4 + (y + k) % 4) for x in range(4) for y in range(4)])
    return snaps


def local(
    velocity,
    synthesis,
    analysis,
    radial_eigen,
    pair_list,
    owner_slot,
    freq_list,
    snap_index,
    block_dft,
    spectra,
):
    row_index = lax.axis_index("row")
    col_index = lax.axis_index("col")
    mine = row_index * 16 + col_index
    moved = lax.all_to_all(to_axial_major(velocity), "col", split_axis=0, concat_axis=0, tiled=True)

    high, low = trig_tables(False)
    synth = jnp.concatenate([high, high, low], axis=2)
    high, low = trig_tables(True)
    anal = jnp.concatenate([high, high, low], axis=2)

    def stacked(matrix):
        high = lax.reduce_precision(matrix, 8, 7)
        low = matrix - high
        high, low = high.astype(bf16), low.astype(bf16)
        return jnp.concatenate([high, high, low], axis=0)

    parity = jnp.arange(2, dtype=jnp.int32)[:, None, None]
    mode_ids = (2 * jnp.arange(HALF, dtype=jnp.int32)[None, :, None] + parity).astype(f32)
    axial_id = mine.astype(f32) * axial_scale
    damping = 1.0 / (
        1.0 + viscosity * (axial_id**2 + mode_ids**2) + radial_eigen[None, None, :]
    )
    damping = damping.reshape(MTH, NR)
    place = jnp.stack([mine, row_index & 1, row_index >> 1, col_index >> 2, col_index & 3])
    lists = pair_lists(pair_list, owner_slot, place)
    terms = [window_terms(freq_list, snap_index[0] + t) for t in range(2)]
    weights = jnp.stack([terms[0][0], terms[0][1], terms[1][0], terms[1][1]], axis=1)
    weights = jnp.concatenate([weights, weights], axis=0)
    weights, damping = lax.optimization_barrier((weights, damping))

    out, keep, send = two_steps(lists, moved, synth, anal, stacked(analysis), stacked(synthesis), damping)

    back = lax.all_to_all(out, "col", split_axis=0, concat_axis=0, tiled=True)
    snaps = route(keep, send)
    retired = retire_old(block_dft, spectra)
    block, spectra_next = admit_new(weights, snaps, block_dft, retired)
    return (from_axial_major(back), block, spectra_next)


def solution(mesh):
    return jax.shard_map(
        local,
        mesh=mesh,
        in_specs=(
            P(None, "col", "row", None),
            P(),
            P(),
            P(),
            P(),
            P(),
            P(),
            P(),
            P(("row", "col"), None, None, None),
            P(("row", "col"), None, None, None, None),
        ),
        out_specs=(
            P(None, "col", "row", None),
            P(("row", "col"), None, None, None),
            P(("row", "col"), None, None, None, None),
        ),
        check_vma=False,
    )
```

```python
import math

import jax
import jax.numpy as jnp
from jax import lax
from jax.experimental import pallas as pl
from jax.experimental.pallas import tpu as pltpu
from jax.sharding import PartitionSpec as P


NBLK = 256
MTH = 512
NTH = 1536
NR = 384
HALF = MTH // 2
QUARTER = NTH // 4

viscosity = 4e-06
axial_scale = 2.0
nonlinear_gain = 0.1

f32 = jnp.float32
bf16 = jnp.bfloat16


SYNTH_WEIGHT = 2.0 / math.sqrt(MTH)
KEEP = math.sqrt(MTH) / NTH
VMEM = pl.BlockSpec(memory_space=pltpu.VMEM)
SMEM = pl.BlockSpec(memory_space=pltpu.SMEM)
HBM = pl.BlockSpec(memory_space=pltpu.HBM)
ANY = pl.BlockSpec(memory_space=pl.ANY)


def in_hbm(array):
    return pltpu.with_memory_space_constraint(array, pltpu.HBM)


def params(mib):
    return pltpu.CompilerParams(vmem_limit_bytes=mib << 20)


def trig_tables(transposed):
    dims = (4, HALF, QUARTER) if transposed else (4, QUARTER, HALF)
    mode_dim, point_dim = (1, 2) if transposed else (2, 1)
    kind = lax.broadcasted_iota(jnp.int32, dims, 0)
    mode = (2 * lax.broadcasted_iota(jnp.int32, dims, mode_dim) + (kind & 1)).astype(f32)
    point = (2 * lax.broadcasted_iota(jnp.int32, dims, point_dim) + 1).astype(f32)
    product = mode * point - jnp.where(kind >= 2, NTH / 2.0, 0.0)
    turn = product - jnp.round(product * (0.5 / NTH)) * (2.0 * NTH)
    quarter = (NTH / 2.0 - jnp.abs(turn)) * (math.pi / NTH)
    square = quarter * quarter
    series = 1.0 / math.factorial(13)
    for power in (11, 9, 7, 5, 3, 1):
        series = (1.0 if power % 4 == 1 else -1.0) / math.factorial(power) + square * series
    table = quarter * series
    high = lax.reduce_precision(table, 8, 7)
    low = table - high
    high, low = high.astype(bf16), low.astype(bf16)
    return high, low


def gather_kernel(src_any, out_any, src, out, sems):
    blocks = [(c, half) for c in range(2) for half in range(2)]
    reads = [
        pltpu.make_async_copy(
            src_any.at[c, pl.ds(half * 16 + 8 * q, 8)], src.at[c, pl.ds(half * 16 + 8 * q, 8)], sems.at[4 * c + 2 * half + q]
        )
        for c, half in blocks
        for q in range(2)
    ]
    for copy in reads:
        copy.start()
    writes = []
    for n, (c, half) in enumerate(blocks):
        reads[2 * n].wait()
        reads[2 * n + 1].wait()
        for parity in range(2):
            block = jnp.stack([src[c, half * 16 + 2 * i + parity] for i in range(8)])
            row = n * 16 + parity * 8
            out[:, row : row + 8, :] = pltpu.einshape("mar->amr", block)
            at = pl.ds(row, 8)
            for q in range(2):
                these = pl.ds(8 * q, 8)
                writes.append(
                    pltpu.make_async_copy(
                        out.at[these, at], out_any.at[these, at], sems.at[8 + 4 * n + 2 * parity + q]
                    )
                )
                writes[-1].start()
    for copy in writes:
        copy.wait()


def to_axial_major(velocity):
    return pl.pallas_call(
        gather_kernel,
        out_shape=pltpu.HBM((16, 64, NR), f32),
        in_specs=[HBM],
        out_specs=HBM,
        scratch_shapes=[
            pltpu.VMEM((2, 32, 16, NR), f32),
            pltpu.VMEM((16, 64, NR), f32),
            pltpu.SemaphoreType.DMA((24,)),
        ],
        compiler_params=params(8),
        cost_estimate=pl.CostEstimate(flops=0, bytes_accessed=2 * 1024 * NR * 4, transcendentals=0),
        name="axial_major",
    )(in_hbm(velocity))


def scatter_kernel(src, out_any, out, sems):
    writes = []
    for n in range(4):
        c, half = n // 2, n % 2
        for parity in range(2):
            row = n * 16 + parity * 8
            moved = pltpu.einshape("amr->mar", src[:, row : row + 8, :])
            for i in range(8):
                out[c, half * 16 + 2 * i + parity] = moved[i]
        for q in range(2):
            at = pl.ds(half * 16 + 8 * q, 8)
            writes.append(pltpu.make_async_copy(out.at[c, at], out_any.at[c, at], sems.at[2 * n + q]))
            writes[-1].start()
    for copy in writes:
        copy.wait()


def from_axial_major(moved):
    return pl.pallas_call(
        scatter_kernel,
        out_shape=jax.ShapeDtypeStruct((2, 32, 16, NR), f32),
        in_specs=[VMEM],
        out_specs=ANY,
        scratch_shapes=[pltpu.VMEM((2, 32, 16, NR), f32), pltpu.SemaphoreType.DMA((8,))],
        compiler_params=params(8),
        cost_estimate=pl.CostEstimate(flops=0, bytes_accessed=2 * 1024 * NR * 4, transcendentals=0),
        name="mode_major",
    )(moved)


def list_kernel(pair_ref, owner_ref, place_ref, count_ref, spot_ref, mode_ref):
    mine, core, z, x, y = (place_ref[i] for i in range(5))

    def eight(b, n):
        for u in range(8):
            mode_ref[n] = b * 8 + u
            n = n + jnp.where(pair_ref[0, b * 8 + u] == mine, 1, 0)
        return n

    def place_one(k, carry):
        i = mode_ref[k]
        slot = owner_ref[i]
        row, col = slot // 32, (slot // 2) & 15
        spot_ref[k] = (
            ((row & 1) ^ core) * 128
            + (((row >> 1) - z) & 3) * 32
            + (((col >> 2) - x) & 3) * 8
            + (((col & 3) - y) & 3) * 2
            + (slot & 1)
        )
        mode_ref[k] = pair_ref[1, i]
        return carry

    count = lax.fori_loop(0, 32, eight, 0)
    count_ref[0] = count
    lax.fori_loop(0, count, place_one, 0)


def pair_lists(pair_list, owner_slot, place):
    return pl.pallas_call(
        list_kernel,
        out_shape=(
            jax.ShapeDtypeStruct((1,), jnp.int32),
            jax.ShapeDtypeStruct((257,), jnp.int32),
            jax.ShapeDtypeStruct((257,), jnp.int32),
        ),
        in_specs=[SMEM] * 3,
        out_specs=[SMEM] * 3,
        compiler_params=params(1),
        cost_estimate=pl.CostEstimate(flops=0, bytes_accessed=8000000, transcendentals=0),
        name="pair_lists",
    )(pair_list.T, owner_slot, place)


def split(value):
    high = value.astype(bf16)
    return high, (value - high.astype(f32)).astype(bf16)


WIDE = 256
REST = NR - WIDE


def steps_kernel(
    count_ref,
    spot_ref,
    mode_ref,
    moved_any,
    synth_any,
    anal_any,
    analysis_any,
    synthesis_any,
    damp_any,
    out_any,
    keep_any,
    send_any,
    state,
    synth_ref,
    anal_ref,
    analysis_ref,
    synthesis_ref,
    damp_ref,
    cols,
    cols_rest,
    phys,
    squares,
    squares_rest,
    rows,
    parcel,
    sems,
):
    def strip(array, part, half):
        return array.at[:, pl.ds((part // 2) * 32 + half * 16 + (part % 2) * 8, 8), :]

    def held(part, half):
        return state.at[part, :, pl.ds(half * 8, 8), :]

    moved_in = [
        [
            pltpu.make_async_copy(strip(moved_any, part, half), held(part, half), sems.at[2 * part + half])
            for half in range(2)
        ]
        for part in range(4)
    ]
    field_out = [
        pltpu.make_async_copy(held(part, half), strip(out_any, part, half), sems.at[2 * part + half])
        for part in range(4)
        for half in range(2)
    ]
    synth_in = [
        pltpu.make_async_copy(synth_any.at[part], synth_ref.at[part], sems.at[8 + part]) for part in range(4)
    ]
    anal_in = [pltpu.make_async_copy(anal_any.at[part], anal_ref.at[part], sems.at[12 + part]) for part in range(4)]
    rest_in = [
        pltpu.make_async_copy(analysis_any, analysis_ref, sems.at[16]),
        pltpu.make_async_copy(damp_any, damp_ref, sems.at[17]),
        pltpu.make_async_copy(synthesis_any, synthesis_ref, sems.at[18]),
    ]
    for part in range(4):
        for copy in moved_in[part]:
            copy.start()
        synth_in[part].start()
    for copy in anal_in + rest_in:
        copy.start()
    parcel[...] = jnp.zeros_like(parcel)

    def store_rows(at, start, value):
        high, low = split(value)
        width = value.shape[1]
        rows[at, start : start + width] = high
        rows[at, NR + start : NR + start + width] = low

    def store_stack(wide, rest, part, size, b, count, band, value):
        high, low = split(value)
        if band == 0:
            wide[part, pl.ds(b, count), :] = high
            wide[part, pl.ds(size + b, count), :] = low
            wide[part, pl.ds(2 * size + b, count), :] = high
        else:
            rest[part, pl.ds(b, count), 0:REST] = high
            rest[part, pl.ds(b, count), REST : 2 * REST] = low

    def against(table, wide, rest, part, size, band):
        if band == 0:
            return jnp.dot(table[part], wide[part], preferred_element_type=f32)
        both = jnp.dot(table[part, :, 0:size], rest[part], preferred_element_type=f32)
        low = jnp.dot(table[part, :, 2 * size : 3 * size], rest[part, :, 0:REST], preferred_element_type=f32)
        return both[:, 0:REST] + both[:, REST:] + low

    def solve(at, matrix, then):
        both = jnp.dot(rows[at, :], matrix[:, 0 : WIDE + 2 * REST], preferred_element_type=f32)
        low = jnp.dot(rows[at, 0:NR], matrix[0:NR, WIDE + 2 * REST :], preferred_element_type=f32)
        then(0, both[:, 0:WIDE] + low)
        then(WIDE, both[:, WIDE:NR] + both[:, NR:])

    bands = ((0, WIDE), (WIDE, REST))

    def step(t):
        for band, (start, width) in enumerate(bands):
            lanes = pl.ds(start, width)
            for part in range(4):
                for b in range(0, HALF, 64):
                    scaled = state[part, pl.ds(b // 16, 4), :, lanes].reshape(64, width) * SYNTH_WEIGHT
                    if part == 0 and b == 0:
                        first_row = lax.broadcasted_iota(jnp.int32, scaled.shape, 0) == 0
                        scaled = jnp.where(first_row, 0.5 * scaled, scaled)
                    store_stack(cols, cols_rest, part, HALF, b, 64, band, scaled)
                phys[part, :, lanes] = against(synth_ref, cols, cols_rest, part, HALF, band)

        if t == 0:
            for copy in anal_in + rest_in:
                copy.wait()
        for band, (start, width) in enumerate(bands):
            lanes = pl.ds(start, width)
            for b in range(0, QUARTER, 32):
                ce, co, se, so = (phys[part, pl.ds(b, 32), lanes] for part in range(4))
                a, b_, s, d = ce + co, ce - co, se + so, se - so
                near, far = a * a + s * s, b_ * b_ + d * d
                near_x, far_x = a * s, b_ * d
                for part, value in enumerate((near + far, near - far, near_x + far_x, near_x - far_x)):
                    store_stack(squares, squares_rest, part, QUARTER, b, 32, band, value)
            for part in range(4):
                folded = against(anal_ref, squares, squares_rest, part, QUARTER, band)
                gain = -nonlinear_gain * KEEP * (2.0 if part < 2 else 4.0)
                if part == 0:
                    first_row = lax.broadcasted_iota(jnp.int32, folded.shape, 0) == 0
                    folded = jnp.where(first_row, 0.0, folded)
                old = state[part, :, :, lanes].reshape(HALF, width)
                store_rows(pl.ds(part * HALF, HALF), start, old + gain * folded)
        for half in range(2):
            at = pl.ds(half * MTH, MTH)

            def damped(start, value):
                store_rows(at, start, value * damp_ref[:, start : start + value.shape[1]])

            solve(at, analysis_ref, damped)
        for half in range(2):

            def placed(start, value):
                width = value.shape[1]
                state[pl.ds(2 * half, 2), :, :, start : start + width] = value.reshape(2, 16, 16, width)

            solve(pl.ds(half * MTH, MTH), synthesis_ref, placed)

            if t == 1:
                for copy in field_out[4 * half : 4 * half + 4]:
                    copy.start()

    def pick(t):
        def one(i, carry):
            mode = mode_ref[i]
            part, group, row = mode & 1, (mode >> 1) >> 4, (mode >> 1) & 15
            dst = spot_ref[i] * 4 + 2 * t
            parcel[pl.ds(dst, 1), :] = state[part, group, pl.ds(row, 1), :]
            parcel[pl.ds(dst + 1, 1), :] = state[part + 2, group, pl.ds(row, 1), :]
            return carry

        lax.fori_loop(0, count_ref[0], one, 0)

    for part in range(4):
        for copy in moved_in[part] + [synth_in[part]]:
            copy.wait()
    for t in range(2):
        step(t)
        pick(t)
    parcel_out = [
        pltpu.make_async_copy(parcel.at[pl.ds(512, 512)], send_any, sems.at[8]),
        pltpu.make_async_copy(parcel.at[pl.ds(0, 512)], keep_any, sems.at[9]),
    ]
    for copy in parcel_out:
        copy.start()
    for copy in field_out + parcel_out:
        copy.wait()


def two_steps(lists, moved, synth, anal, analysis, synthesis, damping):
    return pl.pallas_call(
        steps_kernel,
        out_shape=(
            pltpu.HBM((16, 64, NR), f32),
            pltpu.HBM((512, NR), f32),
            pltpu.HBM((512, NR), f32),
        ),
        in_specs=[SMEM] * 3 + [ANY] + [HBM] * 5,
        out_specs=[HBM, HBM, HBM],
        scratch_shapes=[
            pltpu.VMEM((4, 16, 16, NR), f32),
            pltpu.VMEM((4, QUARTER, 3 * HALF), bf16),
            pltpu.VMEM((4, HALF, 3 * QUARTER), bf16),
            pltpu.VMEM((2 * NR, 2 * NR), bf16),
            pltpu.VMEM((2 * NR, 2 * NR), bf16),
            pltpu.VMEM((MTH, NR), f32),
            pltpu.VMEM((4, 3 * HALF, WIDE), bf16),
            pltpu.VMEM((4, HALF, 2 * REST), bf16),
            pltpu.VMEM((4, QUARTER, NR), f32),
            pltpu.VMEM((4, 3 * QUARTER, WIDE), bf16),
            pltpu.VMEM((4, QUARTER, 2 * REST), bf16),
            pltpu.VMEM((1024, 2 * NR), bf16),
            pltpu.VMEM((1024, NR), f32),
            pltpu.SemaphoreType.DMA((19,)),
        ],
        compiler_params=params(40),
        cost_estimate=pl.CostEstimate(flops=8_000_000_000, bytes_accessed=10_000_000, transcendentals=0),
        name="two_steps",
    )(*lists, moved, *map(in_hbm, (synth, anal, analysis, synthesis, damping)))


def products(lefts, rights, left, right):
    def three(value):
        high = value.astype(bf16).astype(f32)
        middle = (value - high).astype(bf16).astype(f32)
        return high, middle, (value - high - middle).astype(bf16).astype(f32)

    pairs = ((0, 0), (0, 1), (1, 0), (1, 1), (0, 2), (2, 0))
    left[...] = jnp.zeros_like(left)
    right[...] = jnp.zeros_like(right)
    count = len(rights)
    for k in range(count):
        for part in range(2):
            pieces = three(lefts[k][part])
            for p, (i, _) in enumerate(pairs):
                left[p * count + k : p * count + k + 1, part * NR : (part + 1) * NR] = pieces[i]
        pieces = three(rights[k])
        for p, (_, i) in enumerate(pairs):
            right[p * count + k : p * count + k + 1, :] = pieces[i]
    r = right[...].astype(bf16)
    for part in range(2):
        l = left[:, part * NR : (part + 1) * NR].T.astype(bf16)
        yield part, jnp.dot(l, r, preferred_element_type=f32)


def retire_kernel(block_ref, spectra_ref, out_ref, left, right):
    step = pl.program_id(0)
    real, imag = block_ref[0, 0:1, :], block_ref[0, 1:2, :]
    for part, value in products(((real, imag), (imag, -real)), (real, imag), left, right):
        out_ref[step, part] = spectra_ref[0, part] - value


def retire_old(block_dft, spectra):
    return pl.pallas_call(
        retire_kernel,
        out_shape=jax.ShapeDtypeStruct((8, 2, NR, NR), f32),
        grid=(8,),
        in_specs=[
            pl.BlockSpec((1, 2, NR), lambda i: (i, 0, 0)),
            pl.BlockSpec((1, 2, NR, NR), lambda i: (i, 0, 0, 0)),
        ],
        out_specs=VMEM,
        scratch_shapes=[pltpu.VMEM((16, 2 * NR), f32), pltpu.VMEM((16, NR), f32)],
        compiler_params=params(16),
        cost_estimate=pl.CostEstimate(flops=300_000_000, bytes_accessed=19_000_000, transcendentals=0),
        name="retire_old",
    )(block_dft.reshape(8, 2, NR), in_hbm(spectra.reshape(8, 2, NR, NR)))


def admit_kernel(weight_ref, snap_ref, block_ref, retired_ref, sums_ref, out_any, spread, sems):
    real, imag = block_ref[:, 0, :], block_ref[:, 1, :]
    for t in range(2):
        real_w, imag_w = weight_ref[:, 2 * t : 2 * t + 1], weight_ref[:, 2 * t + 1 : 2 * t + 2]
        snap_real, snap_imag = (
            jnp.concatenate(
                [
                    jnp.broadcast_to(snap_ref[slot * 4 + 2 * t + c : slot * 4 + 2 * t + c + 1, :], (4, NR))
                    for slot in range(2)
                ],
                axis=0,
            )
            for c in range(2)
        )
        real, imag = (
            real + real_w * snap_real - imag_w * snap_imag,
            imag + real_w * snap_imag + imag_w * snap_real,
        )
    sums_ref[:, 0, :] = real
    sums_ref[:, 1, :] = imag
    real_cols, imag_cols = real.T, imag.T
    copies = []
    rows = NR // 2
    for i in range(8):
        for half in range(2):
            n = 2 * i + half
            held = n % 8
            if n >= 8:
                copies[n - 8].wait()
            for b in range(0, rows, 32):
                at, here = pl.ds(half * rows + b, 32), pl.ds(b, 32)
                cr = real_cols[half * rows + b : half * rows + b + 32, i : i + 1]
                ci = imag_cols[half * rows + b : half * rows + b + 32, i : i + 1]
                rr, ri = real[i : i + 1, :], imag[i : i + 1, :]
                spread[held, 0, here, :] = retired_ref[i, 0, at, :] + (cr * rr + ci * ri)
                spread[held, 1, here, :] = retired_ref[i, 1, at, :] + (ci * rr - cr * ri)
            copies.append(
                pltpu.make_async_copy(
                    spread.at[held], out_any.at[i, :, pl.ds(half * rows, rows), :], sems.at[n]
                )
            )
            copies[n].start()
    for n in range(8, 16):
        copies[n].wait()


def admit_new(weights, snaps, block_dft, retired):
    sums, out = pl.pallas_call(
        admit_kernel,
        out_shape=(
            jax.ShapeDtypeStruct((8, 2, NR), f32),
            jax.ShapeDtypeStruct((8, 2, NR, NR), f32),
        ),
        in_specs=[VMEM] * 4,
        out_specs=[VMEM, ANY],
        scratch_shapes=[pltpu.VMEM((8, 2, NR // 2, NR), f32), pltpu.SemaphoreType.DMA((16,))],
        compiler_params=params(8),
        cost_estimate=pl.CostEstimate(flops=300_000_000, bytes_accessed=10_000_000, transcendentals=0),
        name="admit_new",
    )(weights, snaps, block_dft.reshape(8, 2, NR), retired)
    return sums.reshape(2, 4, 2, NR), out.reshape(2, 4, 2, NR, NR)


def window_terms(freq_list, snap_now):
    position = snap_now.astype(f32)
    window = 0.54 - 0.46 * jnp.cos(2.0 * math.pi * position / NBLK)
    phase = (freq_list * snap_now % NBLK).astype(f32) * (2.0 * math.pi / NBLK)
    return (window * jnp.cos(phase), -window * jnp.sin(phase))


def route(keep, send):
    rows = [[z * 2 + c for c in range(2)] for z in range(4)]
    got = lax.ppermute(send, "row", [(i, i ^ 1) for i in range(8)])
    z_size = 128
    blocks = [keep[k * z_size : (k + 1) * z_size] + got[k * z_size : (k + 1) * z_size] for k in range(4)]

    def turn(blocks, axis, pairs_of):
        total = blocks[0]
        for k in range(1, 4):
            moved = lax.ppermute(blocks[k], axis, pairs_of(k))
            total = total + moved
        return total

    total = turn(blocks, "row", lambda k: [(rows[z][c], rows[(z + k) % 4][c]) for z in range(4) for c in range(2)])
    blocks = [total[k * 32 : (k + 1) * 32] for k in range(4)]
    total = turn(blocks, "col", lambda k: [(x * 4 + y, (x + k) % 4 * 4 + y) for x in range(4) for y in range(4)])
    blocks = [total[k * 8 : (k + 1) * 8] for k in range(4)]
    return turn(blocks, "col", lambda k: [(x * 4 + y, x * 4 + (y + k) % 4) for x in range(4) for y in range(4)])


def local(
    velocity,
    synthesis,
    analysis,
    radial_eigen,
    pair_list,
    owner_slot,
    freq_list,
    snap_index,
    block_dft,
    spectra,
):
    row_index = lax.axis_index("row")
    col_index = lax.axis_index("col")
    mine = row_index * 16 + col_index
    moved = lax.all_to_all(to_axial_major(velocity), "col", split_axis=0, concat_axis=0, tiled=True)

    high, low = trig_tables(False)
    synth = jnp.concatenate([high, high, low], axis=2)
    high, low = trig_tables(True)
    anal = jnp.concatenate([high, high, low], axis=2)

    def stacked(matrix):
        high = lax.reduce_precision(matrix, 8, 7)
        low = matrix - high
        high, low = high.astype(bf16), low.astype(bf16)
        upper = jnp.concatenate([high, low[:, WIDE:], low[:, :WIDE]], axis=1)
        lower = jnp.concatenate([high, jnp.zeros((NR, NR), bf16)], axis=1)
        return jnp.concatenate([upper, lower], axis=0)

    parity = jnp.arange(2, dtype=jnp.int32)[:, None, None]
    mode_ids = (2 * jnp.arange(HALF, dtype=jnp.int32)[None, :, None] + parity).astype(f32)
    axial_id = mine.astype(f32) * axial_scale
    damping = 1.0 / (
        1.0 + viscosity * (axial_id**2 + mode_ids**2) + radial_eigen[None, None, :]
    )
    damping = damping.reshape(MTH, NR)
    place = jnp.stack([mine, row_index & 1, row_index >> 1, col_index >> 2, col_index & 3])
    lists = pair_lists(pair_list, owner_slot, place)
    terms = [window_terms(freq_list, snap_index[0] + t) for t in range(2)]
    weights = jnp.stack([terms[0][0], terms[0][1], terms[1][0], terms[1][1]], axis=1)
    weights = jnp.concatenate([weights, weights], axis=0)
    weights, damping = lax.optimization_barrier((weights, damping))

    out, keep, send = two_steps(lists, moved, synth, anal, stacked(analysis), stacked(synthesis), damping)

    back = lax.all_to_all(out, "col", split_axis=0, concat_axis=0, tiled=True)
    snaps = route(keep, send)
    retired = retire_old(block_dft, spectra)
    block, spectra_next = admit_new(weights, snaps, block_dft, retired)
    return (from_axial_major(back), block, spectra_next)


def solution(mesh):
    return jax.shard_map(
        local,
        mesh=mesh,
        in_specs=(
            P(None, "col", "row", None),
            P(),
            P(),
            P(),
            P(),
            P(),
            P(),
            P(),
            P(("row", "col"), None, None, None),
            P(("row", "col"), None, None, None, None),
        ),
        out_specs=(
            P(None, "col", "row", None),
            P(("row", "col"), None, None, None),
            P(("row", "col"), None, None, None, None),
        ),
        check_vma=False,
    )
```
